32 devices in a mesh: rep: 4 (over z), fsdp: 4 (over x, core), tp: 2 (over y).
Axes of the slice: x: 2, y: 2, z: 4, core: 2. Of those that a mesh axis runs over, the one named last changes fastest.
Arguments:
- inputs: bfloat16 [32, 128, 2304], P(('rep', 'fsdp')), as said below
- block_seq: int32 [32], replicated, may hold values from 0 to 3, as said below
- block_pos: int32 [32], replicated, may hold values from 0 to 7, as said below
- query_weight: bfloat16 [2304, 2048], P('fsdp', 'tp'), may hold values from -0.0625 to 0.0625
- key_projection_weight: bfloat16 [2304, 1024], P('fsdp', 'tp'), may hold values from -0.0625 to 0.0625
- value_projection_weight: bfloat16 [2304, 1024], P('fsdp', 'tp'), may hold values from -0.125 to 0.125
- out_weight: bfloat16 [2048, 2304], P('tp', 'fsdp'), may hold values from -0.125 to 0.125
- gate_weight: bfloat16 [2304, 9216], P('fsdp', 'tp'), may hold values from -0.125 to 0.125
- up_weight: bfloat16 [2304, 9216], P('fsdp', 'tp'), may hold values from -0.125 to 0.125
- down_weight: bfloat16 [9216, 2304], P('tp', 'fsdp'), may hold values from -0.0625 to 0.0625
- input_gain: bfloat16 [2304], P('fsdp'), may hold values from -0.5 to 0.5
- attention_gain: bfloat16 [2304], P('fsdp'), may hold values from -0.5 to 0.5
- middle_gain: bfloat16 [2304], P('fsdp'), may hold values from -0.5 to 0.5
- output_gain: bfloat16 [2304], P('fsdp'), may hold values from -0.5 to 0.5
- cotangent: bfloat16 [32, 128, 2304], P(('rep', 'fsdp')), may hold values from -6 to 6
Outputs:
- layer_output: bfloat16 [32, 128, 2304], P(('rep', 'fsdp'))
- input_grad: bfloat16 [32, 128, 2304], P(('rep', 'fsdp'))
- query_grad: float32 [2304, 2048], P('fsdp', 'tp')
- key_grad: float32 [2304, 1024], P('fsdp', 'tp')
- value_grad: float32 [2304, 1024], P('fsdp', 'tp')
- out_grad: float32 [2048, 2304], P('tp', 'fsdp')
- gate_grad: float32 [2304, 9216], P('fsdp', 'tp')
- up_grad: float32 [2304, 9216], P('fsdp', 'tp')
- down_grad: float32 [9216, 2304], P('tp', 'fsdp')
- input_gain_grad: float32 [2304], P('fsdp')
- attention_gain_grad: float32 [2304], P('fsdp')
- middle_gain_grad: float32 [2304], P('fsdp')
- output_gain_grad: float32 [2304], P('fsdp')
The draws below stay inside these ranges and needn't reach their ends.
Inputs may be any that keep to these rules, and one draw needn't show every extreme that they name: `inputs`: Activations. `block_seq`: the k-th aligned run of 8 slots holds every block of sequences k * 1 to (k + 1) - 1 exactly once, in any order. `block_pos`: each pair of sequence and position occurs in exactly one slot.
All inputs are finite; a program needn't handle non-finite values.
Results may differ from the reference program's by a relative error of at most 0.025.
Values may be sent and summed in bfloat16 or wider, within the bound.
A program may use at most 320 MiB of HBM per device.

```python
import math
import jax
import jax.numpy as jnp
from jax import lax

MODEL_DIM = 2304
QUERY_HEADS = 8
KEY_VALUE_HEADS = 4
HEAD_SIZE = 256
FF = 9216
BLK = 128
GROUP_BLKS = 8
BLOCKS = 32
SEQ_BLKS = 8
SEQ_GRP = 1


def draw_inputs(key, part):
    base_key, row_key, column_key = jax.random.split(key, 3)
    base_draw = jnp.clip(jax.random.normal(base_key, (BLOCKS, BLK, MODEL_DIM), jnp.float32), -5.0, 5.0)
    row_scale = jnp.exp(jax.random.uniform(row_key, (BLOCKS, BLK, 1), jnp.float32, math.log(0.3), math.log(3.0)))
    column_scale = jnp.exp(jax.random.uniform(column_key, (MODEL_DIM,), jnp.float32, math.log(0.5), math.log(2.0)))
    return (base_draw * row_scale * column_scale).astype(jnp.bfloat16)


def block_items(key):
    query_group_count = BLOCKS // GROUP_BLKS
    group_keys = jax.random.split(jax.random.fold_in(key, 11), query_group_count)
    orders = jax.vmap(lambda one_key: jax.random.permutation(one_key, GROUP_BLKS))(group_keys)
    return orders.astype(jnp.int32)


def draw_block_seq(key, part):
    orders = block_items(key)
    group_ids = jnp.arange(BLOCKS // GROUP_BLKS, dtype=jnp.int32)[:, None]
    return (group_ids * SEQ_GRP + orders // SEQ_BLKS).reshape(-1).astype(jnp.int32)


def draw_block_pos(key, part):
    return (block_items(key) % SEQ_BLKS).reshape(-1).astype(jnp.int32)


def block_scale(own_key, dims, cuts, smallest, high):
    def one(dim, parts):
        draws = jax.random.uniform(jax.random.fold_in(jax.random.fold_in(own_key, 6), dim), (parts,), jnp.float32, smallest / len(cuts), high / len(cuts))
        return jnp.repeat(jnp.exp(draws), dims[dim] // parts).reshape((-1,) + (1,) * (len(dims) - dim - 1))

    level = one(*cuts[0])
    for cut in cuts[1:]:
        level = level * one(*cut)
    return level


def bell_draw(own_key, dims, spread, limit, cuts=(), held_as=jnp.bfloat16):
    entries = spread * jax.random.normal(own_key, dims, jnp.float32)
    if cuts:
        entries = entries * block_scale(own_key, dims, cuts, -0.22, 0.18)
    return jnp.clip(entries, -limit, limit).astype(held_as)


def setup_inputs(seed: int = 0) -> dict:
    streams_of = jax.random.split(jax.random.key(seed), 16)
    inputs = draw_inputs(jax.random.fold_in(streams_of[15], 71), 0)
    block_seq = draw_block_seq(jax.random.fold_in(streams_of[15], 71), 0)
    block_pos = draw_block_pos(jax.random.fold_in(streams_of[15], 71), 0)
    query_weight = bell_draw(streams_of[3], (MODEL_DIM, QUERY_HEADS * HEAD_SIZE), (4 * MODEL_DIM) ** -0.5, 0.0625, ((0, 4), (1, 2)))
    key_projection_weight = bell_draw(streams_of[4], (MODEL_DIM, KEY_VALUE_HEADS * HEAD_SIZE), (4 * MODEL_DIM) ** -0.5, 0.0625, ((0, 4), (1, 2)))
    value_projection_weight = bell_draw(streams_of[5], (MODEL_DIM, KEY_VALUE_HEADS * HEAD_SIZE), MODEL_DIM ** -0.5, 0.125, ((0, 4), (1, 2)))
    out_weight = bell_draw(streams_of[6], (QUERY_HEADS * HEAD_SIZE, MODEL_DIM), (QUERY_HEADS * HEAD_SIZE) ** -0.5, 0.125, ((0, 2), (1, 4)))
    gate_weight = bell_draw(streams_of[7], (MODEL_DIM, FF), MODEL_DIM ** -0.5, 0.125, ((0, 4), (1, 2)))
    up_weight = bell_draw(streams_of[8], (MODEL_DIM, FF), MODEL_DIM ** -0.5, 0.125, ((0, 4), (1, 2)))
    down_weight = bell_draw(streams_of[9], (FF, MODEL_DIM), FF ** -0.5, 0.0625, ((0, 2), (1, 4)))
    input_gain = jnp.clip(jax.random.uniform(streams_of[10], (MODEL_DIM,), jnp.float32, -0.5, 0.5) * block_scale(streams_of[10], (MODEL_DIM,), ((0, 4),), -0.4, 0.0), -0.5, 0.5).astype(jnp.bfloat16)
    attention_gain = jnp.clip(jax.random.uniform(streams_of[11], (MODEL_DIM,), jnp.float32, -0.5, 0.5) * block_scale(streams_of[11], (MODEL_DIM,), ((0, 4),), -0.4, 0.0), -0.5, 0.5).astype(jnp.bfloat16)
    middle_gain = jnp.clip(jax.random.uniform(streams_of[12], (MODEL_DIM,), jnp.float32, -0.5, 0.5) * block_scale(streams_of[12], (MODEL_DIM,), ((0, 4),), -0.4, 0.0), -0.5, 0.5).astype(jnp.bfloat16)
    output_gain = jnp.clip(jax.random.uniform(streams_of[13], (MODEL_DIM,), jnp.float32, -0.5, 0.5) * block_scale(streams_of[13], (MODEL_DIM,), ((0, 4),), -0.4, 0.0), -0.5, 0.5).astype(jnp.bfloat16)
    cotangent = bell_draw(streams_of[14], (BLOCKS, BLK, MODEL_DIM), 1.0, 6.0, ((0, 16),))
    return dict(inputs=inputs, block_seq=block_seq, block_pos=block_pos, query_weight=query_weight, key_projection_weight=key_projection_weight, value_projection_weight=value_projection_weight, out_weight=out_weight, gate_weight=gate_weight, up_weight=up_weight, down_weight=down_weight, input_gain=input_gain, attention_gain=attention_gain, middle_gain=middle_gain, output_gain=output_gain, cotangent=cotangent)


@jax.custom_vjp
def reduced_input(v):
    return lax.optimization_barrier(v.astype(jnp.bfloat16)).astype(jnp.float32)

@jax.custom_vjp
def reduced_gradient(v):
    return v

def low_keep(v):
    return (reduced_input(v), None)

def low_pass(kept, grad):
    return (grad,)

def back_keep(v):
    return (v, None)

def back_low(kept, grad):
    return (reduced_input(grad),)
reduced_input.defvjp(low_keep, low_pass)
reduced_gradient.defvjp(back_keep, back_low)
EPSILON = 1e-06
SOFT_CAP = 50.0

def score_product(left_mat, right_mat):
    return jnp.dot(left_mat, right_mat, preferred_element_type=jnp.float32, precision=lax.Precision.HIGHEST)

def rms_scale(values, gain_vec):
    return values * lax.rsqrt(lax.optimization_barrier(jnp.mean(values * values, axis=-1, keepdims=True)) + EPSILON) * (1.0 + gain_vec)

def rotate(values, positions):
    half_dim = values.shape[-1] // 2
    frequency = jnp.exp(jnp.arange(half_dim, dtype=jnp.float32) * (-2.0 * math.log(10000.0) / values.shape[-1]))
    angles = positions.astype(jnp.float32)[:, None, None] * frequency
    cos_part = jnp.cos(angles)
    sine_part = jnp.sin(angles)
    first_half = values[..., :half_dim]
    second = values[..., half_dim:]
    return jnp.concatenate([first_half * cos_part - second * sine_part, second * cos_part + first_half * sine_part], axis=-1)

def attend_block(packed, key_rotated, value_rot, key_seq, key_pos):
    query_block, query_seq, query_pos = packed
    scores = reduced_gradient(jnp.einsum('rhgd,nhd->hgrn', query_block, key_rotated, precision=lax.Precision.HIGHEST) * HEAD_SIZE ** (-0.5))
    capped = SOFT_CAP * jnp.tanh(scores / SOFT_CAP)
    allowed = (query_seq[:, None] == key_seq[None, :]) & (key_pos[None, :] <= query_pos[:, None])
    expw = jnp.where(allowed, jnp.exp(capped), 0.0)
    weight_sum = lax.optimization_barrier(jnp.sum(expw, axis=-1))
    weighted = reduced_gradient(jnp.einsum('hgrn,nhd->rhgd', reduced_input(expw), value_rot, precision=lax.Precision.HIGHEST))
    return weighted / jnp.transpose(weight_sum, (2, 0, 1))[..., None]

def attend_query_group(packed):
    query_group, key_group, value_group, seq_group, pos_group = packed
    block_total = query_group.shape[0] // BLK
    query_blocks = query_group.reshape((block_total, BLK) + query_group.shape[1:])
    seq_blocks = seq_group.reshape(block_total, BLK)
    pos_blocks = pos_group.reshape(block_total, BLK)
    block_fn = jax.checkpoint(lambda inner: attend_block(inner, key_group, value_group, seq_group, pos_group))
    return lax.map(block_fn, (query_blocks, seq_blocks, pos_blocks)).reshape(query_group.shape)

def reference(inputs, block_seq, block_pos, query_weight, key_projection_weight, value_projection_weight, out_weight, gate_weight, up_weight, down_weight, input_gain, attention_gain, middle_gain, output_gain, cotangent):
    token_sequence = jnp.repeat(block_seq, BLK).astype(jnp.int32)
    token_position = (block_pos[:, None] * BLK + jnp.arange(BLK, dtype=jnp.int32)[None, :]).reshape(-1).astype(jnp.int32)
    source_rows = inputs.reshape(-1, MODEL_DIM).astype(jnp.float32)
    query_group_count = BLOCKS // GROUP_BLKS
    group_length = GROUP_BLKS * BLK
    group_width = QUERY_HEADS // KEY_VALUE_HEADS

    def layer_fn(source, query_w, key_matrix, value_matrix, out_w, gate_w, up_w, down_w, gain_in, gain_attn, gain_mid, gain_out):
        attention_input = reduced_input(rms_scale(source, gain_in))
        query_lin = reduced_gradient(score_product(attention_input, query_w)).reshape(-1, QUERY_HEADS, HEAD_SIZE)
        key_linear = reduced_gradient(score_product(attention_input, key_matrix)).reshape(-1, KEY_VALUE_HEADS, HEAD_SIZE)
        value_reduced = reduced_input(reduced_gradient(score_product(attention_input, value_matrix))).reshape(-1, KEY_VALUE_HEADS, HEAD_SIZE)
        query_rotated = reduced_input(rotate(query_lin, token_position))
        key_rotated = reduced_input(rotate(key_linear, token_position))
        attended_rows = lax.map(jax.checkpoint(attend_query_group), (query_rotated.reshape(query_group_count, group_length, KEY_VALUE_HEADS, group_width, HEAD_SIZE), key_rotated.reshape(query_group_count, group_length, KEY_VALUE_HEADS, HEAD_SIZE), value_reduced.reshape(query_group_count, group_length, KEY_VALUE_HEADS, HEAD_SIZE), token_sequence.reshape(query_group_count, group_length), token_position.reshape(query_group_count, group_length))).reshape(-1, QUERY_HEADS * HEAD_SIZE)
        attn_raw = reduced_gradient(score_product(reduced_input(reduced_gradient(attended_rows)), out_w))
        h_mid = source + rms_scale(attn_raw, gain_attn)
        ffn_in = reduced_input(rms_scale(h_mid, gain_mid))
        gate = reduced_gradient(score_product(ffn_in, gate_w))
        up_val = reduced_gradient(score_product(ffn_in, up_w))
        hidden = reduced_input(jax.nn.gelu(gate, approximate=True) * up_val)
        ffn_raw = reduced_gradient(score_product(hidden, down_w))
        return h_mid + rms_scale(ffn_raw, gain_out)
    result, pullback = jax.vjp(layer_fn, source_rows, query_weight.astype(jnp.float32), key_projection_weight.astype(jnp.float32), value_projection_weight.astype(jnp.float32), out_weight.astype(jnp.float32), gate_weight.astype(jnp.float32), up_weight.astype(jnp.float32), down_weight.astype(jnp.float32), input_gain.astype(jnp.float32), attention_gain.astype(jnp.float32), middle_gain.astype(jnp.float32), output_gain.astype(jnp.float32))
    grads = pullback(cotangent.reshape(-1, MODEL_DIM).astype(jnp.float32))
    layer_output = result.astype(jnp.bfloat16).reshape(inputs.shape)
    input_grad = grads[0].astype(jnp.bfloat16).reshape(inputs.shape)
    return (layer_output, input_grad, grads[1], grads[2], grads[3], grads[4], grads[5], grads[6], grads[7], grads[8], grads[9], grads[10], grads[11])
```

```python
import math

import jax
import jax.numpy as jnp
from jax import lax
from jax.sharding import PartitionSpec as P

HEAD_SIZE = 256
BLK = 128
EPSILON = 1e-06
SOFT_CAP = 50.0
BF = jnp.bfloat16
F32 = jnp.float32


def rms_scale(values, gain_vec):
    return (
        values
        * lax.rsqrt(jnp.mean(values * values, axis=-1, keepdims=True) + EPSILON)
        * (1.0 + gain_vec)
    )


def angles_of(positions):
    half_dim = HEAD_SIZE // 2
    frequency = jnp.exp(
        jnp.arange(half_dim, dtype=F32) * (-2.0 * math.log(10000.0) / HEAD_SIZE)
    )
    angles = positions.astype(F32)[:, None, None] * frequency
    return jnp.cos(angles), jnp.sin(angles)


def rotate(values, cos_part, sine_part):
    half_dim = HEAD_SIZE // 2
    first = values[..., :half_dim]
    second = values[..., half_dim:]
    return jnp.concatenate(
        [first * cos_part - second * sine_part, second * cos_part + first * sine_part], axis=-1
    )


def gated_unit(gate_val, up_val):
    return jax.nn.gelu(gate_val, approximate=True) * up_val


def matmul(left_mat, right_mat):
    return jnp.dot(left_mat, right_mat, preferred_element_type=F32)


def outer_sum(left_mat, right_mat):
    return lax.dot_general(
        left_mat, right_mat, (((0,), (0,)), ((), ())), preferred_element_type=F32
    )


def back_product(grad_mat, weight):
    return lax.dot_general(
        grad_mat, weight, (((1,), (1,)), ((), ())), preferred_element_type=F32
    )


def swap(value, axis, bit):
    count = lax.axis_size(axis)
    return lax.ppermute(value, axis, [(i, i ^ bit) for i in range(count)])


def rows_at(value, start, rows):
    return lax.dynamic_slice_in_dim(value, start, rows, 0)


class Plane:
    def __init__(self):
        self.n = lax.axis_size("fsdp")
        self.reps = lax.axis_size("rep")
        self.f = lax.axis_index("fsdp")
        self.quick = self.n == 4 and self.reps == 4
        self.half = lax.axis_index("rep") % 2
        index = jnp.arange(self.n, dtype=jnp.int32)
        self.order = (index ^ self.f) if self.quick else index

    def _both_halves(self, mine):
        other = swap(mine, "rep", 1)
        first = self.half == 0
        return jnp.concatenate([jnp.where(first, mine, other), jnp.where(first, other, mine)], axis=-2)

    def place(self, pieces, axis, dtype=None):
        size = pieces[0].shape[axis]
        shape = list(pieces[0].shape)
        shape[axis] *= self.n
        dtype = dtype or pieces[0].dtype
        whole = jnp.zeros(shape, dtype)
        for r, piece in enumerate(pieces):
            whole = lax.dynamic_update_slice_in_dim(
                whole, piece.astype(dtype), (self.f ^ r) * size, axis
            )
        return whole

    def gather_rows(self, shard):
        if not self.quick:
            return lax.all_gather(shard, "fsdp", axis=0, tiled=True)
        rows = shard.shape[0] // 2
        near = swap(shard, "fsdp", 1)
        across = self._both_halves(swap(rows_at(shard, self.half * rows, rows), "fsdp", 2))
        return self.place([shard, near, across, swap(across, "fsdp", 1)], 0)

    def exchange(self, piece_of, axis, dtype=None):
        f, n = self.f, self.n
        if not self.quick:
            pieces = jnp.stack([piece_of(d, 0, None) for d in range(n)])
            got = lax.all_to_all(pieces, "fsdp", 0, 0, tiled=True)
            got = got.astype(dtype or got.dtype)
            return jnp.concatenate([got[d] for d in range(n)], axis=axis)
        own = piece_of(f, 0, None)
        rows = own.shape[0] // 2
        near = swap(piece_of(f ^ 1, 0, None), "fsdp", 1)
        across = jnp.stack(
            [piece_of(f ^ 2, self.half * rows, rows), piece_of(f ^ 3, self.half * rows, rows)]
        )
        across = self._both_halves(swap(across, "fsdp", 2))
        return self.place([own, near, across[0], swap(across[1], "fsdp", 1)], axis, dtype)

    def gather_tokens(self, rows):
        if not self.quick:
            return lax.all_gather(rows, "fsdp", axis=0, tiled=True)
        near = swap(rows, "fsdp", 1)
        across = swap(rows, "fsdp", 2)
        return jnp.concatenate([rows, near, across, swap(across, "fsdp", 1)])

    def scatter_sum(self, pieces):
        if not self.quick:
            whole = jnp.concatenate([p.astype(BF) for p in pieces])
            return lax.psum_scatter(whole, "fsdp", scatter_dimension=0, tiled=True).astype(F32)
        got = swap(jnp.concatenate([pieces[1].astype(BF), pieces[3].astype(BF)]), "fsdp", 1)
        rows = pieces[0].shape[0]
        own = pieces[0] + got[:rows].astype(F32)
        across = pieces[2] + got[rows:].astype(F32)
        return own + swap(across.astype(BF), "fsdp", 2).astype(F32)

    def pieces(self, whole):
        rows = whole.shape[0] // self.n
        if not self.quick:
            return [whole[r * rows : (r + 1) * rows] for r in range(self.n)]
        return [rows_at(whole, (self.f ^ r) * rows, rows) for r in range(self.n)]

    def split(self, whole):
        rows = whole.shape[0] // self.n
        return [whole[r * rows : (r + 1) * rows] for r in range(self.n)]

    def sum_groups(self, own):
        if not self.quick:
            return lax.psum(own.astype(BF), "rep").astype(F32)
        z = lax.axis_index("rep")
        rows = own.shape[0] // 2
        lo, hi = z & 1, z // 2
        mine = rows_at(own, lo * rows, rows)
        away = rows_at(own, (1 - lo) * rows, rows).astype(BF)
        mine = mine + swap(away, "rep", 1).astype(F32)
        quarter = rows // 2
        keep = rows_at(mine, hi * quarter, quarter)
        away = rows_at(mine, (1 - hi) * quarter, quarter).astype(BF)
        done = (keep + swap(away, "rep", 2).astype(F32)).astype(BF)
        other = swap(done, "rep", 2)
        part = jnp.concatenate([jnp.where(hi == 0, done, other), jnp.where(hi == 0, other, done)])
        other = swap(part, "rep", 1)
        return jnp.concatenate(
            [jnp.where(lo == 0, part, other), jnp.where(lo == 0, other, part)]
        ).astype(F32)


def sum_heads(partial):
    low = partial.astype(BF)
    if lax.axis_size("tp") != 2:
        return lax.psum(low, "tp").astype(F32)
    return low.astype(F32) + swap(low, "tp", 1).astype(F32)


def on_device(
    inputs,
    block_seq,
    block_pos,
    query_weight,
    key_projection_weight,
    value_projection_weight,
    out_weight,
    gate_weight,
    up_weight,
    down_weight,
    input_gain,
    attention_gain,
    middle_gain,
    output_gain,
    cotangent,
):
    plane = Plane()
    n, f = plane.n, plane.f
    blocks_dev, _, model_width = inputs.shape
    row_count = blocks_dev * BLK
    own_slot = lax.axis_index(("rep", "fsdp")) * blocks_dev
    base_slot = lax.axis_index("rep") * (n * blocks_dev)
    in_block = jnp.arange(BLK, dtype=jnp.int32)

    def token_meta(slots):
        seq = jnp.repeat(jnp.take(block_seq, slots), BLK)
        pos = (jnp.take(block_pos, slots)[:, None] * BLK + in_block[None, :]).reshape(-1)
        return seq, pos

    block_ids = jnp.arange(blocks_dev, dtype=jnp.int32)
    own_seq, own_pos = token_meta(own_slot + block_ids)
    all_seq, all_pos = token_meta(
        base_slot + (plane.order[:, None] * blocks_dev + block_ids[None, :]).reshape(-1)
    )
    allowed = (own_seq[:, None] == all_seq[None, :]) & (all_pos[None, :] <= own_pos[:, None])
    score_scale = HEAD_SIZE ** (-0.5)
    source = inputs.reshape(row_count, model_width).astype(F32)
    out_rows = cotangent.reshape(row_count, model_width).astype(F32)

    gain_shard = jnp.stack([input_gain, attention_gain, middle_gain, output_gain])
    if plane.quick:
        near = swap(gain_shard, "fsdp", 1)
        pair = jnp.concatenate([gain_shard, near])
        gathered = jnp.concatenate([pair, swap(pair, "fsdp", 2)]).reshape(4, 4, -1)
        gains = jnp.take(gathered, plane.order, axis=0)
    else:
        gains = lax.all_gather(gain_shard, "fsdp", axis=0)
    gains = gains.transpose(1, 0, 2).reshape(4, model_width).astype(F32)
    gain_input, gain_attn, gain_middle, gain_output = gains

    full_query = plane.gather_rows(query_weight)
    full_kv = plane.gather_rows(
        jnp.concatenate([key_projection_weight, value_projection_weight], axis=1)
    )
    full_out = plane.gather_rows(out_weight.T)
    kv_width = key_projection_weight.shape[1]
    query_local = full_query.shape[1] // HEAD_SIZE
    kv_local = kv_width // HEAD_SIZE
    group_width = query_local // kv_local

    ff_width = gate_weight.shape[1] // n

    def slice_of(weight):
        def piece_of(d, lo, rows):
            return lax.dynamic_slice(
                weight, (lo, d * ff_width), (rows or weight.shape[0], ff_width)
            )

        return plane.exchange(piece_of, 0)

    gate_w = slice_of(gate_weight)
    up_w = slice_of(up_weight)
    down_w = slice_of(down_weight.T)

    attention_input = rms_scale(source, gain_input).astype(BF)
    query_lin = matmul(attention_input, full_query).reshape(row_count, query_local, HEAD_SIZE)
    kv_lin = matmul(attention_input, full_kv)
    key_linear = kv_lin[:, :kv_width].reshape(row_count, kv_local, HEAD_SIZE)
    value_reduced = kv_lin[:, kv_width:].astype(BF)
    cos_part, sine_part = angles_of(own_pos)
    query_rotated = (
        rotate(query_lin, cos_part, sine_part)
        .astype(BF)
        .reshape(row_count, kv_local, group_width, HEAD_SIZE)
    )
    key_rotated = rotate(key_linear, cos_part, sine_part).astype(BF).reshape(row_count, kv_width)
    kv_all = plane.gather_tokens(jnp.concatenate([key_rotated, value_reduced], axis=1))
    key_all = kv_all[:, :kv_width].reshape(-1, kv_local, HEAD_SIZE)
    value_all = kv_all[:, kv_width:].reshape(-1, kv_local, HEAD_SIZE)

    def weights_of(queries, keys):
        scores = (
            jnp.einsum("rhgd,nhd->hgrn", queries, keys, preferred_element_type=F32) * score_scale
        )
        squashed = jnp.tanh(scores / SOFT_CAP)
        return jnp.where(allowed, jnp.exp(SOFT_CAP * squashed), 0.0), squashed

    expw, _ = weights_of(query_rotated, key_all)
    weight_sum = jnp.sum(expw, axis=-1)
    weighted = jnp.einsum(
        "hgrn,nhd->rhgd", expw.astype(BF), value_all, preferred_element_type=F32
    )
    sum_rows = jnp.transpose(weight_sum, (2, 0, 1))[..., None]
    attended_rows = weighted / sum_rows
    attended_low = attended_rows.reshape(row_count, query_local * HEAD_SIZE).astype(BF)
    attn_raw = sum_heads(back_product(attended_low, full_out))
    h_mid = source + rms_scale(attn_raw, gain_attn)

    ffn_in = rms_scale(h_mid, gain_middle).astype(BF)
    ffn_all = lax.all_gather(ffn_in, ("rep", "fsdp"), axis=0, tiled=True)
    ffn_group = plane.gather_tokens(ffn_in)
    gate_val = matmul(ffn_group, gate_w)
    up_val = matmul(ffn_group, up_w)
    hidden_low = gated_unit(gate_val, up_val).astype(BF)
    ffn_raw = sum_heads(plane.scatter_sum(plane.split(back_product(hidden_low, down_w))))
    layer_output = (h_mid + rms_scale(ffn_raw, gain_output)).astype(BF).reshape(inputs.shape)

    _, output_norm_back = jax.vjp(rms_scale, ffn_raw, gain_output)
    ffn_raw_grad, output_dgain = output_norm_back(out_rows)
    ffn_raw_low = ffn_raw_grad.astype(BF)
    raw_all = lax.all_gather(ffn_raw_low, ("rep", "fsdp"), axis=0, tiled=True)
    raw_group = plane.gather_tokens(ffn_raw_low)
    hidden_grad = matmul(raw_group, down_w)
    _, gated_back = jax.vjp(gated_unit, gate_val, up_val)
    gate_back, up_back = gated_back(hidden_grad)
    ffn_in_grad = sum_heads(
        plane.scatter_sum(
            plane.split(
                back_product(gate_back.astype(BF), gate_w) + back_product(up_back.astype(BF), up_w)
            )
        )
    )
    _, middle_norm_back = jax.vjp(rms_scale, h_mid, gain_middle)
    mid_grad, middle_dgain = middle_norm_back(ffn_in_grad)
    h_grad = out_rows + mid_grad

    gate_every = matmul(ffn_all, gate_w)
    up_every = matmul(ffn_all, up_w)
    hidden_every = gated_unit(gate_every, up_every).astype(BF)
    _, every_back = jax.vjp(gated_unit, gate_every, up_every)
    gate_every_back, up_every_back = every_back(matmul(raw_all, down_w))

    def owners(grad):
        rows = grad.shape[0] // n

        def piece_of(d, lo, count):
            return rows_at(grad, d * rows + lo, count or rows)

        return plane.exchange(piece_of, 1, F32)

    down_grad = owners(outer_sum(raw_all, hidden_every).astype(BF)).T
    gate_grad = owners(outer_sum(ffn_all, gate_every_back.astype(BF)).astype(BF))
    up_grad = owners(outer_sum(ffn_all, up_every_back.astype(BF)).astype(BF))

    _, attn_norm_back = jax.vjp(rms_scale, attn_raw, gain_attn)
    attn_raw_grad, attention_dgain = attn_norm_back(h_grad)
    attn_raw_low = attn_raw_grad.astype(BF)
    out_grad = plane.sum_groups(
        plane.scatter_sum(plane.pieces(outer_sum(attn_raw_low, attended_low)))
    ).T
    attended_grad = (
        matmul(attn_raw_low, full_out)
        .astype(BF)
        .reshape(row_count, kv_local, group_width, HEAD_SIZE)
    )
    attended_grad_f = attended_grad.astype(F32)
    weighted_grad = (attended_grad_f / sum_rows).astype(BF)
    sum_grad = (
        -jnp.transpose(jnp.sum(attended_grad_f * attended_rows, axis=-1), (1, 2, 0)) / weight_sum
    )
    expw, squashed = weights_of(*lax.optimization_barrier((query_rotated, key_all)))
    prob_grad = jnp.einsum(
        "rhgd,nhd->hgrn", weighted_grad, value_all, preferred_element_type=F32
    )
    score_grad = (expw * (prob_grad + sum_grad[..., None]) * (1.0 - squashed * squashed)).astype(BF)
    query_acc = (
        jnp.einsum("hgrn,nhd->rhgd", score_grad, key_all, preferred_element_type=F32) * score_scale
    )
    key_acc = (
        jnp.einsum("hgrn,rhgd->nhd", score_grad, query_rotated, preferred_element_type=F32)
        * score_scale
    )
    value_acc = jnp.einsum(
        "hgrn,rhgd->nhd", expw.astype(BF), weighted_grad, preferred_element_type=F32
    )
    kv_grad = plane.scatter_sum(
        plane.split(
            jnp.concatenate(
                [key_acc.reshape(-1, kv_width), value_acc.reshape(-1, kv_width)], axis=1
            )
        )
    )
    query_lin_grad = (
        rotate(query_acc.reshape(row_count, query_local, HEAD_SIZE), cos_part, -sine_part)
        .reshape(row_count, query_local * HEAD_SIZE)
        .astype(BF)
    )
    key_lin_grad = (
        rotate(kv_grad[:, :kv_width].reshape(row_count, kv_local, HEAD_SIZE), cos_part, -sine_part)
        .reshape(row_count, kv_width)
        .astype(BF)
    )
    kv_lin_grad = jnp.concatenate([key_lin_grad, kv_grad[:, kv_width:].astype(BF)], axis=1)
    query_grad = plane.sum_groups(
        plane.scatter_sum(plane.pieces(outer_sum(attention_input, query_lin_grad)))
    )
    kv_weight_grad = plane.sum_groups(
        plane.scatter_sum(plane.pieces(outer_sum(attention_input, kv_lin_grad)))
    )
    attn_in_grad = sum_heads(
        back_product(query_lin_grad, full_query) + back_product(kv_lin_grad, full_kv)
    )
    _, input_norm_back = jax.vjp(rms_scale, source, gain_input)
    source_grad, input_dgain = input_norm_back(attn_in_grad)
    input_grad = (h_grad + source_grad).astype(BF).reshape(inputs.shape)

    dgains = jnp.stack([input_dgain, attention_dgain, middle_dgain, output_dgain])
    dgains = jnp.sum(lax.all_gather(dgains, ("rep", "fsdp"), axis=0), axis=0)
    shard = model_width // n
    dgains = lax.dynamic_slice(dgains, (0, f * shard), (4, shard))
    return (
        layer_output,
        input_grad,
        query_grad,
        kv_weight_grad[:, :kv_width],
        kv_weight_grad[:, kv_width:],
        out_grad,
        gate_grad,
        up_grad,
        down_grad,
        dgains[0],
        dgains[1],
        dgains[2],
        dgains[3],
    )


def solution(mesh):
    tokens = P(("rep", "fsdp"), None, None)
    columns = P("fsdp", "tp")
    rows = P("tp", "fsdp")
    vector = P("fsdp")
    return jax.shard_map(
        on_device,
        mesh=mesh,
        in_specs=(tokens, P(), P(), columns, columns, columns, rows, columns, columns, rows)
        + (vector,) * 4
        + (tokens,),
        out_specs=(tokens, tokens, columns, columns, columns, rows, columns, columns, rows)
        + (vector,) * 4,
        check_vma=False,
    )
```
